32 devices in a mesh: row: 8 (over y, x, core), col: 4 (over z).
Axes of the slice: x: 2, y: 2, z: 4, core: 2. Of those that a mesh axis runs over, the one named last changes fastest.
Arguments:
- corner: bfloat16 [1024, 1024], P('col'), may hold values from -6 to 6
- edge_up: bfloat16 [1024, 36, 128], P('col', None, 'row'), may hold values from -0.1875 to 0.1875
- edge_left: bfloat16 [1024, 36, 1024], P('row', None, 'col'), may hold values from -0.1875 to 0.1875
- doubled: bfloat16 [1296, 1296], replicated, may hold values from -0.15625 to 0.15625
- panel: bfloat16 [36, 1024, 512], P(None, 'col', 'row'), may hold values from -0.03125 to 0.03125
Outputs:
- corner_slab: bfloat16 [36, 36, 128, 1024], P(None, None, 'row', 'col')
- panel_product: bfloat16 [36, 128, 512], P(None, 'row', 'col')
- gram: float32 [512, 512], P('row', 'col')
The draws below stay inside these ranges and needn't reach their ends.
All inputs are finite; a program needn't handle non-finite values.
Results may differ from the reference program's by a relative error of at most 0.009.
Values may be sent and summed in bfloat16 or wider, within the bound.
A program may use at most 256 MiB of HBM per device.

```python
import jax
import jax.numpy as jnp
from jax import lax

CHI = 1024
DL = 36
SLAB_DEV = 16
ALPHA = 128
PANEL = 512
N_ROW = 8


def levels(rng, dims, shards, smallest, top_value):
    gain = 1.0
    for dim, parts in shards:
        heights = jax.random.uniform(jax.random.fold_in(jax.random.fold_in(rng, 6), dim), (parts,), jnp.float32, smallest / len(shards), top_value / len(shards))
        gain = gain * jnp.repeat(jnp.exp(heights), dims[dim] // parts).reshape((-1,) + (1,) * (len(dims) - 1 - dim))
    return gain


def bell_draw(own_key, dims, width, bound, shards=(), held_as=jnp.bfloat16):
    entries = width * jax.random.normal(own_key, dims, jnp.float32)
    if shards:
        entries = entries * levels(own_key, dims, shards, -0.22, 0.18)
    return jnp.clip(entries, -bound, bound).astype(held_as)


def setup_inputs(seed: int = 0) -> dict:
    arg_keys = jax.random.split(jax.random.key(seed), 6)
    corner = bell_draw(arg_keys[0], (CHI, CHI), 1.0, 6.0, ((0, 4),))
    edge_up = bell_draw(arg_keys[1], (CHI, DL, ALPHA), CHI ** -0.5, 0.1875, ((0, 4), (2, 8)))
    edge_left = bell_draw(arg_keys[2], (CHI, DL, CHI), CHI ** -0.5, 0.1875, ((0, 8), (2, 4)))
    doubled = bell_draw(arg_keys[3], (DL * DL, DL * DL), (DL * DL) ** -0.5, 0.15625)
    panel = bell_draw(arg_keys[4], (DL, CHI, PANEL), (CHI * DL) ** -0.5, 0.03125, ((1, 4), (2, 8)))
    return dict(corner=corner, edge_up=edge_up, edge_left=edge_left, doubled=doubled, panel=panel)


def reference(corner, edge_up, edge_left, doubled, panel):
    quad = doubled.astype(jnp.float32).reshape(DL, DL, DL, DL)
    corner_edge = lax.dot_general(edge_up.astype(jnp.float32), corner.astype(jnp.float32), (((0,), (0,)), ((), ())), precision=lax.Precision.HIGHEST, preferred_element_type=jnp.float32).astype(jnp.bfloat16)
    blocks = corner_edge.reshape(DL, N_ROW, SLAB_DEV, CHI).transpose(1, 0, 2, 3)
    left_wide = edge_left.astype(jnp.float32)
    panel_wide = panel.astype(jnp.float32)

    def one_block(block_rows):
        grown = lax.dot_general(block_rows.astype(jnp.float32), left_wide, (((2,), (0,)), ((), ())), precision=lax.Precision.HIGHEST, preferred_element_type=jnp.float32).astype(jnp.bfloat16)
        slab_block = lax.dot_general(quad, grown.astype(jnp.float32), (((0, 1), (0, 2)), ((), ())), precision=lax.Precision.HIGHEST, preferred_element_type=jnp.float32).astype(jnp.bfloat16)
        product = lax.dot_general(slab_block.astype(jnp.float32), panel_wide, (((1, 3), (0, 1)), ((), ())), precision=lax.Precision.HIGHEST, preferred_element_type=jnp.float32).astype(jnp.bfloat16)
        return slab_block, product

    slabs, products = lax.map(one_block, blocks)
    corner_slab = slabs.transpose(1, 2, 0, 3, 4).reshape(DL, DL, ALPHA, CHI)
    panel_product = products.transpose(1, 0, 2, 3).reshape(DL, ALPHA, PANEL)
    wide_product = panel_product.astype(jnp.float32)
    gram = lax.dot_general(wide_product, wide_product, (((0, 1), (0, 1)), ((), ())), precision=lax.Precision.HIGHEST, preferred_element_type=jnp.float32) / (ALPHA * DL)
    return corner_slab, panel_product, gram
```

```python
import jax
import jax.numpy as jnp
from jax import lax
from jax.experimental import pallas as pl
from jax.experimental.pallas import tpu as pltpu
from jax.sharding import PartitionSpec as P

BF = jnp.bfloat16
F32 = jnp.float32
MESH = pl.DeviceIdType.MESH
VLIM = 62


def remote(src, dst, send_sem, recv_sem, device):
    return pltpu.make_async_remote_copy(
        src_ref=src,
        dst_ref=dst,
        send_sem=send_sem,
        recv_sem=recv_sem,
        device_id=device,
        device_id_type=MESH,
    )


def enter(devices):
    barrier = pltpu.get_barrier_semaphore()
    for device in devices:
        pl.semaphore_signal(barrier, inc=1, device_id=device, device_id_type=MESH)
    pl.semaphore_wait(barrier, len(devices))


def zero_one(mask):
    return jnp.where(mask, 1.0, 0.0).astype(BF)


def slab_kernel(
    up, corner, left, doubled, panel, slab, partial,
    every, grown, site, plain, edge, ups, corners, spread, staged,
    sends, recvs, own_sems, zs, zr, cs, cr, in_sems,
):
    dl, delta, lanes = left.shape[0], left.shape[1], 128
    dk, alpha = slab.shape[0], slab.shape[2]
    rows, gamma = up.shape
    halves = left.shape[2] // lanes
    step = every.shape[1]
    groups = dl // step
    n_left, n_all = halves * groups, halves * groups + groups
    q = panel.shape[1]
    cut = step // 2
    pad = edge.shape[0] // alpha
    pairs, pieces = alpha // 2, 3
    piece = dk * dl // pieces
    r, c = lax.axis_index("row"), lax.axis_index("col")
    core, x, y = r % 2, (r // 2) % 2, r // 4
    r_core, r_x, r_y = r + 1 - 2 * core, r + 2 - 4 * x, r + 4 - 8 * y
    r_xy = r_x + 4 - 8 * y
    to_core, to_x, to_y = (r_core, c), (r_x, c), (r_y, c)
    half_rows = gamma // 2

    local = [
        pltpu.make_async_copy(up, ups.at[c], in_sems.at[0]),
        pltpu.make_async_copy(corner, corners.at[c], in_sems.at[1]),
        pltpu.make_async_copy(doubled, plain, in_sems.at[2]),
    ]
    own = {}
    base = pl.multiple_of(r * delta, delta)
    for n in range(n_all):
        if n < n_left:
            h, g = n // groups, n % groups
            own[n] = [
                pltpu.make_async_copy(
                    left.at[pl.ds(g * step, step), :, pl.ds(h * lanes, lanes)],
                    every.at[n, :, pl.ds(base, delta), :],
                    own_sems.at[n, 0],
                )
            ]
        else:
            g = n - n_left
            own[n] = [
                pltpu.make_async_copy(
                    panel.at[pl.ds(g * step, step), :, pl.ds(h * lanes, lanes)],
                    every.at[n, :, pl.ds(pl.multiple_of(r * delta + h * q, q), q), :],
                    own_sems.at[n, h],
                )
                for h in range(halves)
            ]
    local[0].start()
    local[1].start()
    for n in range(n_all):
        for copy in own[n]:
            copy.start()
        if n == 2:
            local[2].start()
    enter([to_core, to_x, to_y] + [(r, (c + d) % 4) for d in (1, 2, 3)])

    def move(kind, n, owner, lo, size, device):
        ref = every.at[n, pl.ds(lo, size), pl.ds(pl.multiple_of(owner * delta, delta), delta), :]
        return remote(ref, ref, sends.at[kind, n], recvs.at[kind, n], device)

    def first(n):
        for copy in own[n]:
            copy.wait()
        for kind, device in ((0, to_x), (1, to_y), (2, to_core)):
            move(kind, n, r, 0, step, device).start()

    def arrived(kind, n, owner, lo, size):
        move(kind, n, owner, lo, size, to_core).wait_recv()

    def half_of(owner, which):
        return corners.at[owner, pl.ds(pl.multiple_of(which * half_rows, half_rows), half_rows), :]

    def along(owner, there):
        way = (there > c).astype(jnp.int32)
        part = half_of(owner, core)
        return [
            remote(ups.at[owner], ups.at[owner], zs.at[0, way, owner], zr.at[0, owner], (r, there)),
            remote(part, part, zs.at[1, way, owner], zr.at[1, owner], (r, there)),
        ]

    def across(owner, which):
        part = half_of(owner, which)
        return remote(part, part, cs.at[owner], cr.at[owner], to_core)

    def inside(p):
        return (p >= 0) & (p < 4)

    def hop(d):
        for sign in (-1, 1):
            owner, there = c + sign * d, c - sign

            @pl.when(inside(owner))
            def _():
                for copy in along(owner, there):
                    copy.wait_recv()
                across(owner, core).start()

                @pl.when(inside(there))
                def _():
                    for copy in along(owner, there):
                        copy.start()

    def others(act):
        for d in (1, 2, 3):
            for sign in (-1, 1):
                owner, there = c + sign * d, c - sign

                @pl.when(inside(owner))
                def _():
                    act(owner, there)

    def mark():
        @pl.loop(0, 12)
        def _(b):
            at = b * lanes + lax.broadcasted_iota(jnp.int32, (1, lanes), 1)
            l = jnp.floor((at.astype(F32) + 0.5) * (1.0 / pad)).astype(jnp.int32)
            k = at - pad * l
            target = jnp.where((k < dk) & (l < dl), k * dl + l, -1)
            row = lax.broadcasted_iota(jnp.int32, (dk * dl, lanes), 0)
            grown[b, 0 : dk * dl, :] = zero_one(row == target)

        row = lax.broadcasted_iota(jnp.int32, spread.shape, 0)
        col = lax.broadcasted_iota(jnp.int32, spread.shape, 1)
        a = jnp.floor((row.astype(F32) + 0.5) * (1.0 / pad)).astype(jnp.int32)
        spread[...] = zero_one(((row - pad * a) * alpha + a == col) & (row - pad * a < dk))

    def turn(lo, hi):
        marks = jnp.concatenate([grown[b, 0 : dk * dl, :] for b in range(12)], axis=1)[:, : dl * pad]
        for i in range(lo, hi, 256):
            w = min(256, hi - i)
            site[i : i + w, :] = lax.dot_general(
                plain[:, i : i + w], marks, (((0,), (0,)), ((), ())), preferred_element_type=F32
            ).astype(BF)

    def make_edge():
        width = 256
        for b in range(corner.shape[1] // width):
            lhs = jnp.concatenate([ups[p] for p in range(4)], axis=1)
            rhs = corners[:, :, b * width : (b + 1) * width].reshape(4 * gamma, width)
            t = jnp.dot(lhs, rhs, preferred_element_type=F32).astype(BF)
            edge[:, b * width : (b + 1) * width] = jnp.dot(
                spread[...], t, preferred_element_type=F32
            ).astype(BF)

    def grow(n0, n1):
        @pl.loop(n0 * (step // 2), n1 * (step // 2))
        def _(u):
            n, m = u // (step // 2), u % (step // 2)
            rhs = jnp.concatenate([every[n, 2 * m], every[n, 2 * m + 1]], axis=1)
            acc = jnp.dot(edge[...], rhs, preferred_element_type=F32)
            at = pl.multiple_of((u % (dl // 2)) * 2 * pad, 16)
            for a in range(alpha):
                t = acc[a * pad : (a + 1) * pad]
                grown[a, pl.ds(at, 2 * pad), :] = jnp.concatenate(
                    [t[:, :lanes], t[:, lanes:]], axis=0
                ).astype(BF)

    def mix(pc, lo, hi):
        @pl.loop(lo, hi)
        def _(p):
            rhs = jnp.concatenate([grown[2 * p], grown[2 * p + 1]], axis=1)
            acc = jnp.dot(
                site[pc * piece : (pc + 1) * piece, :], rhs, preferred_element_type=F32
            ).astype(BF)
            staged[2 * p] = acc[:, :lanes]
            staged[2 * p + 1] = acc[:, lanes:]

    def lay(pc, h):
        @pl.loop(0, piece // 16)
        def _(g):
            t = staged[:, pl.ds(pl.multiple_of(g * 16, 16), 16), :].astype(F32)
            slab_rows = jnp.swapaxes(t, 0, 1).astype(BF)
            for half in range(4):
                ij = pc * piece + g * 16 + half * 4
                slab[ij // dl, pl.ds(ij % dl, 4), :, h * lanes : (h + 1) * lanes] = slab_rows[
                    half * 4 : half * 4 + 4
                ]

    def product(g):
        lhs = jnp.concatenate(
            [slab[:, g * step + j].reshape(rows, halves * lanes) for j in range(step)], axis=1
        )
        parts = []
        for j in range(step):
            t = every[n_left + g, j].reshape(8, halves, q, lanes)
            parts += [t[:, h].reshape(8 * q, lanes) for h in range(halves)]
        term = lax.dot_general(
            lhs, jnp.concatenate(parts, axis=1), (((1,), (1,)), ((), ())), preferred_element_type=F32
        )
        if g == 0:
            partial[...] = term
        else:
            partial[...] += term

    for copy in local[:2]:
        copy.wait()
    for there in (c + 1, c - 1):

        @pl.when(inside(there))
        def _():
            for copy in along(c, there):
                copy.start()

    ahead = 3
    for n in range(ahead):
        first(n)
    work = {
        0: [mark],
        1: [lambda: local[2].wait(), lambda: turn(0, 512)],
        2: [lambda: hop(1), lambda: turn(512, 1024)],
        3: [lambda: turn(1024, dk * dl)],
        4: [lambda: hop(2)],
        5: [
            lambda: hop(3),
            lambda: others(lambda owner, there: across(owner, 1 - core).wait_recv()),
            make_edge,
            lambda: grow(0, 2),
        ],
        6: [lambda: grow(2, 5)],
        7: [lambda: grow(5, 6), lambda: mix(0, 0, 4)],
        8: [lambda: mix(0, 4, pairs), lambda: lay(0, 0)],
        9: [lambda: mix(1, 0, pairs), lambda: lay(1, 0)],
        10: [lambda: mix(2, 0, pairs), lambda: lay(2, 0)],
        11: [lambda: grow(6, 9)],
        12: [lambda: grow(9, 11)],
        13: [lambda: grow(11, 12), lambda: mix(0, 0, 4)],
        14: [lambda: mix(0, 4, pairs), lambda: lay(0, 1)],
        15: [lambda: mix(1, 0, pairs), lambda: lay(1, 1)],
        16: [lambda: mix(2, 0, pairs), lambda: lay(2, 1)],
        17: [lambda: product(0), lambda: product(1), lambda: product(2)],
        18: [lambda: product(3), lambda: product(4)],
        19: [lambda: product(5)],
    }
    for s in range(n_all + 2):
        if s < n_all:
            arrived(0, s, r_x, 0, step)
            move(4, s, r_x, cut, step - cut, to_y).start()
            move(5, s, r_x, 0, step, to_core).start()
            arrived(1, s, r_y, 0, step)
            move(3, s, r_y, 0, cut, to_x).start()
            move(6, s, r_y, 0, step, to_core).start()
        if s + ahead < n_all:
            first(s + ahead)
        if 1 <= s <= n_all:
            arrived(3, s - 1, r_xy, 0, cut)
            move(7, s - 1, r_xy, 0, cut, to_core).start()
            arrived(4, s - 1, r_xy, cut, step - cut)
            move(8, s - 1, r_xy, cut, step - cut, to_core).start()
        if s >= 2:
            for kind, lo, size in ((2, 0, step), (5, 0, step), (6, 0, step), (7, 0, cut), (8, cut, step - cut)):
                arrived(kind, s - 2, r_core, lo, size)
        for act in work[s]:
            act()

    @pl.loop(0, n_all)
    def _(n):
        for kind, size in enumerate((step, step, step, cut, step - cut, step, step, cut, step - cut)):
            move(kind, n, r, 0, size, to_core).wait_send()

    for there in (c + 1, c - 1):

        @pl.when(inside(there))
        def _():
            for copy in along(c, there):
                copy.wait_send()

    def sent(owner, there):
        across(owner, core).wait_send()

        @pl.when(inside(there))
        def _():
            for copy in along(owner, there):
                copy.wait_send()

    others(sent)


def make_slab(edge_up, corner, edge_left, doubled, panel):
    gamma, dk, alpha = edge_up.shape
    delta, dl, beta = edge_left.shape
    q = panel.shape[2]
    rows, total, pad, step = dk * alpha, 8 * delta, 40, 6
    n_all = (beta // 128 + 1) * (dl // step)
    vmem, any_space = pl.BlockSpec(memory_space=pltpu.VMEM), pl.BlockSpec(memory_space=pl.ANY)
    dma = pltpu.SemaphoreType.DMA
    return pl.pallas_call(
        slab_kernel,
        out_shape=(
            jax.ShapeDtypeStruct((dl, dl, alpha, beta), BF),
            jax.ShapeDtypeStruct((rows, 8 * q), F32),
        ),
        in_specs=[any_space] * 5,
        out_specs=(vmem, vmem),
        scratch_shapes=[
            pltpu.VMEM((n_all, step, total, 128), BF),
            pltpu.VMEM((alpha, dl * pad, 128), BF),
            pltpu.VMEM((dl * dl, dl * pad), BF),
            pltpu.VMEM((dk * dl, dl * dl), BF),
            pltpu.VMEM((alpha * pad, total), BF),
            pltpu.VMEM((4, rows, gamma), BF),
            pltpu.VMEM((4, gamma, total), BF),
            pltpu.VMEM((alpha * pad, rows), BF),
            pltpu.VMEM((alpha, dl * dl // 3, 128), BF),
            dma((9, n_all)),
            dma((9, n_all)),
            dma((n_all, 2)),
            dma((2, 2, 4)),
            dma((2, 4)),
            dma((4,)),
            dma((4,)),
            dma((3,)),
        ],
        compiler_params=pltpu.CompilerParams(
            collective_id=0, has_side_effects=True, vmem_limit_bytes=VLIM * 2**20
        ),
        name="slab",
    )(
        edge_up.transpose(1, 2, 0).reshape(rows, gamma),
        corner,
        edge_left.transpose(1, 0, 2),
        doubled,
        panel.transpose(0, 2, 1),
    )


def finish_kernel(total_rows, partial, cols, gram, sent, got, wide, tiles, landed, zs, zr, rs, rr):
    r, c = lax.axis_index("row"), lax.axis_index("col")
    z = [(c + d) % 4 for d in (1, 2, 3)]
    others = [(r + d) % 8 for d in range(1, 8)]
    enter([(r, p) for p in z] + [(p, c) for p in others])
    for p in range(4):
        sent[p] = partial[:, p * 128 : (p + 1) * 128].astype(BF)
    out = [remote(sent.at[z[d]], got.at[d], zs.at[0, d], zr.at[0, d], (r, z[d])) for d in range(3)]
    for copy in out:
        copy.start()
    mine = partial[:, pl.ds(pl.multiple_of(c * 128, 128), 128)]
    for d in range(3):
        out[d].wait_recv()
        mine += got[d].astype(F32)
    mine = mine.astype(BF)
    wide[c] = mine
    cols[...] = mine
    back = [remote(wide.at[c], wide.at[c], zs.at[1, d], zr.at[1, d], (r, z[d])) for d in range(3)]
    for copy in back:
        copy.start()
    for copy in back:
        copy.wait_recv()
    for p in range(4):
        prod = lax.dot_general(
            wide[p], mine, (((0,), (0,)), ((), ())), preferred_element_type=F32
        ) / total_rows
        tiles[2 * p] = prod[:64].astype(BF)
        tiles[2 * p + 1] = prod[64:].astype(BF)
    spread = [
        remote(tiles.at[others[d]], landed.at[d], rs.at[d], rr.at[d], (others[d], c))
        for d in range(7)
    ]
    for copy in spread:
        copy.start()
    total = tiles[r].astype(F32)
    for d in range(7):
        spread[d].wait_recv()
        total += landed[d].astype(F32)
    gram[...] = total
    for copy in out + back + spread:
        copy.wait_send()


def finish(partial, total_rows):
    rows = partial.shape[0]
    vmem = pl.BlockSpec(memory_space=pltpu.VMEM)
    dma = pltpu.SemaphoreType.DMA

    def body(*refs):
        finish_kernel(total_rows, *refs)

    return pl.pallas_call(
        body,
        out_shape=(
            jax.ShapeDtypeStruct((rows, 128), BF),
            jax.ShapeDtypeStruct((64, 128), F32),
        ),
        in_specs=[vmem],
        out_specs=(vmem, vmem),
        scratch_shapes=[
            pltpu.VMEM((4, rows, 128), BF),
            pltpu.VMEM((3, rows, 128), BF),
            pltpu.VMEM((4, rows, 128), BF),
            pltpu.VMEM((8, 64, 128), BF),
            pltpu.VMEM((7, 64, 128), BF),
            dma((2, 3)),
            dma((2, 3)),
            dma((7,)),
            dma((7,)),
        ],
        compiler_params=pltpu.CompilerParams(
            collective_id=1, has_side_effects=True, vmem_limit_bytes=16 * 2**20
        ),
        name="finish",
    )(partial)


def general(corner, edge_up, edge_left, doubled, panel):
    dl, alpha_local = edge_up.shape[1], edge_up.shape[2]
    quad = doubled.reshape(dl, dl, dl, dl)
    partials = lax.dot_general(
        edge_up, corner, (((0,), (0,)), ((), ())), preferred_element_type=F32
    )
    corner_edge = lax.psum(partials, "col").astype(BF)
    grown = lax.dot_general(
        corner_edge,
        lax.all_gather(edge_left, "row", axis=0, tiled=True),
        (((2,), (0,)), ((), ())),
        preferred_element_type=F32,
    ).astype(BF)
    slab = lax.dot_general(
        quad, grown, (((0, 1), (0, 2)), ((), ())), preferred_element_type=F32
    ).astype(BF)
    partial_product = lax.dot_general(
        slab,
        lax.all_gather(panel, "row", axis=2, tiled=True),
        (((1, 3), (0, 1)), ((), ())),
        preferred_element_type=F32,
    )
    own_cols = lax.psum_scatter(partial_product, "col", scatter_dimension=2, tiled=True).astype(BF)
    rows_all = lax.all_gather(own_cols, "col", axis=2, tiled=True)
    total_rows = dl * alpha_local * lax.axis_size("row")
    gram = lax.psum_scatter(
        (
            lax.dot_general(
                rows_all, own_cols, (((0, 1), (0, 1)), ((), ())), preferred_element_type=F32
            )
            / total_rows
        ).astype(BF),
        "row",
        scatter_dimension=0,
        tiled=True,
    ).astype(F32)
    return (slab, own_cols, gram)


def local(corner, edge_up, edge_left, doubled, panel):
    n_row, n_col = lax.axis_size("row"), lax.axis_size("col")
    if (n_row, n_col) != (8, 4):
        return general(corner, edge_up, edge_left, doubled, panel)
    dl, alpha = edge_up.shape[1], edge_up.shape[2]
    slab, partial = make_slab(edge_up, corner, edge_left, doubled, panel)
    cols, gram = finish(partial, dl * alpha * n_row)
    return (slab, cols.reshape(dl, alpha, -1), gram)


def solution(mesh):
    in_specs = (
        P("col", None),
        P("col", None, "row"),
        P("row", None, "col"),
        P(),
        P(None, "col", "row"),
    )
    out_specs = (P(None, None, "row", "col"), P(None, "row", "col"), P("row", "col"))
    return jax.shard_map(local, mesh=mesh, in_specs=in_specs, out_specs=out_specs, check_vma=False)
```

```python
import jax
import jax.numpy as jnp
from jax import lax
from jax.experimental import pallas as pl
from jax.experimental.pallas import tpu as pltpu
from jax.sharding import PartitionSpec as P

BF = jnp.bfloat16
F32 = jnp.float32
MESH = pl.DeviceIdType.MESH
VLIM = 53


def remote(src, dst, send_sem, recv_sem, device):
    return pltpu.make_async_remote_copy(
        src_ref=src,
        dst_ref=dst,
        send_sem=send_sem,
        recv_sem=recv_sem,
        device_id=device,
        device_id_type=MESH,
    )


def enter(devices):
    barrier = pltpu.get_barrier_semaphore()
    for device in devices:
        pl.semaphore_signal(barrier, inc=1, device_id=device, device_id_type=MESH)
    pl.semaphore_wait(barrier, len(devices))


def zero_one(mask):
    return jnp.where(mask, 1.0, 0.0).astype(BF)


def slab_kernel(
    total_rows, up, corner, left, doubled, panel, slab, cols, gram,
    every, grown, site, rest, edge, ups, corners, spread, staged, sums, zout, zgot, wide, tiles, landed,
    sends, recvs, own_sems, zs, zr, cs, cr, in_sems, ss, sr, gs, gr, ts, tr,
):
    dl, delta, lanes = left.shape[0], left.shape[1], 128
    dk, alpha = slab.shape[0], slab.shape[2]
    rows, gamma = up.shape
    halves = left.shape[2] // lanes
    step = every.shape[1]
    groups = dl // step
    n_left, n_all = halves * groups, halves * groups + groups
    q = panel.shape[1]
    cut = step // 2
    pad = edge.shape[0] // alpha
    pairs, pieces = alpha // 2, 3
    piece = dk * dl // pieces
    r, c = lax.axis_index("row"), lax.axis_index("col")
    core, x, y = r % 2, (r // 2) % 2, r // 4
    r_core, r_x, r_y = r + 1 - 2 * core, r + 2 - 4 * x, r + 4 - 8 * y
    r_xy = r_x + 4 - 8 * y
    to_core, to_x, to_y = (r_core, c), (r_x, c), (r_y, c)
    half_rows = gamma // 2
    share, block = rows // 4, 2 * q
    p_own, p_x, p_y, p_xy = r // 2, r_x // 2, r_y // 2, r_xy // 2
    peers = [lax.rem(c + d, 4) for d in (1, 2, 3)]
    row_peers = [lax.rem(r + d, 8) for d in range(1, 8)]

    local = [
        pltpu.make_async_copy(up, ups.at[c], in_sems.at[0]),
        pltpu.make_async_copy(corner, corners.at[c], in_sems.at[1]),
    ]
    flat = slab.reshape(dk * dl, alpha, halves * lanes)
    tall, wide_lanes = doubled.shape[0], halves * lanes
    full = doubled.shape[2] // wide_lanes
    for b in range(full):
        src = doubled.at[:, :, pl.ds(b * wide_lanes, wide_lanes)]
        local.append(pltpu.make_async_copy(src, flat.at[pl.ds(b * tall, tall)], in_sems.at[2 + b]))
    over = doubled.shape[2] - full * wide_lanes
    src = doubled.at[:, :, pl.ds(full * wide_lanes, over)]
    local.append(pltpu.make_async_copy(src, rest, in_sems.at[2 + full]))
    own = {}
    base = pl.multiple_of(r * delta, delta)
    for n in range(n_all):
        if n < n_left:
            h, g = n // groups, n % groups
            own[n] = [
                pltpu.make_async_copy(
                    left.at[pl.ds(g * step, step), :, pl.ds(h * lanes, lanes)],
                    every.at[n, :, pl.ds(base, delta), :],
                    own_sems.at[n, 0],
                )
            ]
        else:
            g = n - n_left
            own[n] = [
                pltpu.make_async_copy(
                    panel.at[pl.ds(g * step, step), :, pl.ds(h * lanes, lanes)],
                    every.at[n, :, pl.ds(pl.multiple_of(r * delta + h * q, q), q), :],
                    own_sems.at[n, h],
                )
                for h in range(halves)
            ]
    local[0].start()
    local[1].start()
    for n in range(n_all):
        for copy in own[n]:
            copy.start()
        if n == 2:
            for copy in local[2:]:
                copy.start()
    enter([(p, c) for p in row_peers] + [(r, p) for p in peers])

    def move(kind, n, owner, lo, size, device):
        ref = every.at[n, pl.ds(lo, size), pl.ds(pl.multiple_of(owner * delta, delta), delta), :]
        return remote(ref, ref, sends.at[kind, n], recvs.at[kind, n], device)

    def first(n):
        for copy in own[n]:
            copy.wait()
        for kind, device in ((0, to_x), (1, to_y), (2, to_core)):
            move(kind, n, r, 0, step, device).start()

    def arrived(kind, n, owner, lo, size):
        move(kind, n, owner, lo, size, to_core).wait_recv()

    def half_of(owner, which):
        return corners.at[owner, pl.ds(pl.multiple_of(which * half_rows, half_rows), half_rows), :]

    def along(owner, there):
        way = (there > c).astype(jnp.int32)
        part = half_of(owner, core)
        return [
            remote(ups.at[owner], ups.at[owner], zs.at[0, way, owner], zr.at[0, owner], (r, there)),
            remote(part, part, zs.at[1, way, owner], zr.at[1, owner], (r, there)),
        ]

    def across(owner, which):
        part = half_of(owner, which)
        return remote(part, part, cs.at[owner], cr.at[owner], to_core)

    def inside(p):
        return (p >= 0) & (p < 4)

    def hop(d):
        for sign in (-1, 1):
            owner, there = c + sign * d, c - sign

            @pl.when(inside(owner))
            def _():
                for copy in along(owner, there):
                    copy.wait_recv()
                across(owner, core).start()

                @pl.when(inside(there))
                def _():
                    for copy in along(owner, there):
                        copy.start()

    def others(act):
        for d in (1, 2, 3):
            for sign in (-1, 1):
                owner, there = c + sign * d, c - sign

                @pl.when(inside(owner))
                def _():
                    act(owner, there)

    def mark():
        @pl.loop(0, 12)
        def _(b):
            at = b * lanes + lax.broadcasted_iota(jnp.int32, (1, lanes), 1)
            l = jnp.floor((at.astype(F32) + 0.5) * (1.0 / pad)).astype(jnp.int32)
            k = at - pad * l
            target = jnp.where((k < dk) & (l < dl), k * dl + l, -1)
            row = lax.broadcasted_iota(jnp.int32, (dk * dl, lanes), 0)
            grown[b, 0 : dk * dl, :] = zero_one(row == target)

        row = lax.broadcasted_iota(jnp.int32, spread.shape, 0)
        col = lax.broadcasted_iota(jnp.int32, spread.shape, 1)
        a = jnp.floor((row.astype(F32) + 0.5) * (1.0 / pad)).astype(jnp.int32)
        spread[...] = zero_one(((row - pad * a) * alpha + a == col) & (row - pad * a < dk))

    def turn(lo, hi):
        marks = jnp.concatenate([grown[b, 0 : dk * dl, :] for b in range(12)], axis=1)[:, : dl * pad]
        for b in range(lo, hi):
            i = b * wide_lanes
            w = wide_lanes if b < full else over
            part = flat[b * tall : (b + 1) * tall] if b < full else rest[...]
            site[i : i + w, :] = lax.dot_general(
                part.reshape(dk * dl, w), marks, (((0,), (0,)), ((), ())), preferred_element_type=F32
            ).astype(BF)

    def make_edge():
        width = 256
        for b in range(corner.shape[1] // width):
            lhs = jnp.concatenate([ups[p] for p in range(4)], axis=1)
            rhs = corners[:, :, b * width : (b + 1) * width].reshape(4 * gamma, width)
            t = jnp.dot(lhs, rhs, preferred_element_type=F32).astype(BF)
            edge[:, b * width : (b + 1) * width] = jnp.dot(
                spread[...], t, preferred_element_type=F32
            ).astype(BF)

    def grow(n0, n1):
        @pl.loop(n0 * (step // 2), n1 * (step // 2))
        def _(u):
            n, m = u // (step // 2), u % (step // 2)
            rhs = jnp.concatenate([every[n, 2 * m], every[n, 2 * m + 1]], axis=1)
            acc = jnp.dot(edge[...], rhs, preferred_element_type=F32)
            at = pl.multiple_of((u % (dl // 2)) * 2 * pad, 16)
            for a in range(alpha):
                t = acc[a * pad : (a + 1) * pad]
                grown[a, pl.ds(at, 2 * pad), :] = jnp.concatenate(
                    [t[:, :lanes], t[:, lanes:]], axis=0
                ).astype(BF)

    def mix(pc, lo, hi):
        @pl.loop(lo, hi)
        def _(p):
            rhs = jnp.concatenate([grown[2 * p], grown[2 * p + 1]], axis=1)
            acc = jnp.dot(
                site[pc * piece : (pc + 1) * piece, :], rhs, preferred_element_type=F32
            ).astype(BF)
            staged[2 * p] = acc[:, :lanes]
            staged[2 * p + 1] = acc[:, lanes:]

    def lay(pc, h):
        @pl.loop(0, piece // 16)
        def _(g):
            t = staged[:, pl.ds(pl.multiple_of(g * 16, 16), 16), :]
            slab_rows = jnp.swapaxes(t, 0, 1)
            for half in range(4):
                ij = pc * piece + g * 16 + half * 4
                slab[ij // dl, pl.ds(ij % dl, 4), :, h * lanes : (h + 1) * lanes] = slab_rows[
                    half * 4 : half * 4 + 4
                ]

    def product(blocks, g0, g1):
        if g0 == 0:
            for p in blocks:
                sums[p] = jnp.zeros((rows, block), F32)

        @pl.loop(g0, g1)
        def _(g):
            lhs = jnp.concatenate(
                [slab[:, g * step + j].reshape(rows, halves * lanes) for j in range(step)], axis=1
            )
            rhs = []
            for p in blocks:
                parts = []
                for j in range(step):
                    at = pl.ds(pl.multiple_of(p * 2 * delta, delta), 2 * delta)
                    t = every[n_left + g, j, at].reshape(2, halves, q, lanes)
                    parts += [t[:, h].reshape(block, lanes) for h in range(halves)]
                rhs.append(jnp.concatenate(parts, axis=1))
            term = lax.dot_general(
                lhs, jnp.concatenate(rhs, axis=0), (((1,), (1,)), ((), ())), preferred_element_type=F32
            )
            for i, p in enumerate(blocks):
                sums[p] += term[:, i * block : (i + 1) * block]

    def portion(ref, p, owner):
        return ref.at[p, pl.ds(pl.multiple_of(owner * share, 16), share), :]

    def out_copy(p, d):
        return remote(
            portion(zout, p, peers[d]), zgot.at[d, p], ss.at[d, p], sr.at[d, p], (r, peers[d])
        )

    def back_copy(p, d, owner):
        part = portion(wide, p, owner)
        return remote(part, part, gs.at[d, p], gr.at[d, p], (r, peers[d]))

    def scatter(blocks):
        for p in blocks:
            zout[p] = sums[p].astype(BF)
            for d in range(3):
                out_copy(p, d).start()

    def total(blocks):
        for p in blocks:
            mine = pl.ds(pl.multiple_of(c * share, 16), share)
            acc = sums[p, mine, :]
            for d in range(3):
                out_copy(p, d).wait_recv()
                acc += zgot[d, p].astype(F32)
            wide[p, mine, :] = acc.astype(BF)
            for d in range(3):
                back_copy(p, d, c).start()

    def gathered(blocks):
        for p in blocks:
            for d in range(3):
                back_copy(p, d, peers[2 - d]).wait_recv()

    def far(n):
        arrived(3, n, r_xy, 0, cut)
        move(7, n, r_xy, 0, cut, to_core).start()
        arrived(4, n, r_xy, cut, step - cut)
        move(8, n, r_xy, cut, step - cut, to_core).start()

    def far_core(n):
        arrived(7, n, r_core, 0, cut)
        arrived(8, n, r_core, cut, step - cut)

    def near_core(n):
        for kind in (2, 5, 6):
            arrived(kind, n, r_core, 0, step)

    for copy in local[:2]:
        copy.wait()
    for there in (c + 1, c - 1):

        @pl.when(inside(there))
        def _():
            for copy in along(c, there):
                copy.start()

    ahead = 3
    for n in range(ahead):
        first(n)
    work = {
        0: [mark],
        1: [lambda: hop(1), lambda: [copy.wait() for copy in local[2:]], lambda: turn(0, 2)],
        2: [lambda: turn(2, 4)],
        3: [lambda: hop(2), lambda: turn(4, full + 1)],
        4: [],
        5: [
            lambda: hop(3),
            lambda: others(lambda owner, there: across(owner, 1 - core).wait_recv()),
            make_edge,
            lambda: grow(0, 2),
        ],
        6: [lambda: grow(2, 5)],
        7: [lambda: grow(5, 6), lambda: mix(0, 0, 4)],
        8: [lambda: mix(0, 4, pairs), lambda: lay(0, 0)],
        9: [lambda: mix(1, 0, pairs), lambda: lay(1, 0)],
        10: [lambda: mix(2, 0, pairs), lambda: lay(2, 0)],
        11: [lambda: grow(6, 9)],
        12: [lambda: grow(9, 11)],
        13: [lambda: grow(11, 12), lambda: mix(0, 0, 4)],
        14: [lambda: mix(0, 4, pairs), lambda: lay(0, 1)],
        15: [lambda: mix(1, 0, pairs), lambda: lay(1, 1)],
        16: [lambda: mix(2, 0, pairs), lambda: lay(2, 1)],
        17: [],
    }
    for s in range(n_all):
        arrived(0, s, r_x, 0, step)
        move(4, s, r_x, cut, step - cut, to_y).start()
        move(5, s, r_x, 0, step, to_core).start()
        arrived(1, s, r_y, 0, step)
        move(3, s, r_y, 0, cut, to_x).start()
        move(6, s, r_y, 0, step, to_core).start()
        if s < n_left:
            first(s + ahead)
        if s == n_left - 1:
            for n in range(n_left + ahead, n_all):
                first(n)
        if 1 <= s <= n_left:
            far(s - 1)
        if 2 <= s < n_left + 2:
            near_core(s - 2)
            far_core(s - 2)
        for act in work[s]:
            act()
    for n in range(n_left, n_all):
        near_core(n)
    product([p_own], 0, groups)
    scatter([p_own])
    product([p_x, p_y], 0, groups)
    scatter([p_x, p_y])
    total([p_own])
    far(n_left)
    for g in range(groups):
        if g + 1 < groups:
            far(n_left + g + 1)
        far_core(n_left + g)
        product([p_xy], g, g + 1)
        if g == groups - 2:
            total([p_x, p_y])
    scatter([p_xy])
    total([p_xy])
    gathered([p_own, p_x, p_y, p_xy])
    mine = wide[c]
    cols[...] = mine
    part = tiles.shape[1]
    for p in range(4):
        prod = lax.dot_general(
            wide[p], mine, (((0,), (0,)), ((), ())), preferred_element_type=F32
        ) / total_rows
        tiles[2 * p] = prod[:part].astype(BF)
        tiles[2 * p + 1] = prod[part:].astype(BF)
    tile_out = [
        remote(tiles.at[row_peers[d]], landed.at[d], ts.at[d], tr.at[d], (row_peers[d], c))
        for d in range(7)
    ]
    for copy in tile_out:
        copy.start()
    whole = tiles[r].astype(F32)
    for d in range(7):
        tile_out[d].wait_recv()
        whole += landed[d].astype(F32)
    gram[...] = whole

    for copy in tile_out:
        copy.wait_send()
    for p in range(4):
        for d in range(3):
            out_copy(p, d).wait_send()
            back_copy(p, d, c).wait_send()

    @pl.loop(0, n_all)
    def _(n):
        for kind, size in enumerate((step, step, step, cut, step - cut, step, step, cut, step - cut)):
            move(kind, n, r, 0, size, to_core).wait_send()

    for there in (c + 1, c - 1):

        @pl.when(inside(there))
        def _():
            for copy in along(c, there):
                copy.wait_send()

    def sent(owner, there):
        across(owner, core).wait_send()

        @pl.when(inside(there))
        def _():
            for copy in along(owner, there):
                copy.wait_send()

    others(sent)


def make_slab(edge_up, corner, edge_left, doubled, panel, total_rows):
    gamma, dk, alpha = edge_up.shape
    delta, dl, beta = edge_left.shape
    q = panel.shape[2]
    rows, total, pad, step = dk * alpha, 8 * delta, 40, 6
    n_all = (beta // 128 + 1) * (dl // step)
    vmem, any_space = pl.BlockSpec(memory_space=pltpu.VMEM), pl.BlockSpec(memory_space=pl.ANY)
    dma = pltpu.SemaphoreType.DMA

    def body(*refs):
        slab_kernel(total_rows, *refs)

    return pl.pallas_call(
        body,
        out_shape=(
            pltpu.VMEM((dl, dl, alpha, beta), BF),
            pltpu.VMEM((rows, 2 * q), BF),
            pltpu.VMEM((q, 2 * q), F32),
        ),
        in_specs=[any_space] * 5,
        out_specs=(vmem, vmem, vmem),
        scratch_shapes=[
            pltpu.VMEM((n_all, step, total, 128), BF),
            pltpu.VMEM((alpha, dl * pad, 128), BF),
            pltpu.VMEM((dl * dl, dl * pad), BF),
            pltpu.VMEM((dk * dl // 16, 16, (dl * dl) % beta), BF),
            pltpu.VMEM((alpha * pad, total), BF),
            pltpu.VMEM((4, rows, gamma), BF),
            pltpu.VMEM((4, gamma, total), BF),
            pltpu.VMEM((alpha * pad, rows), BF),
            pltpu.VMEM((alpha, dl * dl // 3, 128), BF),
            pltpu.VMEM((4, rows, 2 * q), F32),
            pltpu.VMEM((4, rows, 2 * q), BF),
            pltpu.VMEM((3, 4, rows // 4, 2 * q), BF),
            pltpu.VMEM((4, rows, 2 * q), BF),
            pltpu.VMEM((8, q, 2 * q), BF),
            pltpu.VMEM((7, q, 2 * q), BF),
            dma((9, n_all)),
            dma((9, n_all)),
            dma((n_all, 2)),
            dma((2, 2, 4)),
            dma((2, 4)),
            dma((4,)),
            dma((4,)),
            dma((8,)),
            dma((3, 4)),
            dma((3, 4)),
            dma((3, 4)),
            dma((3, 4)),
            dma((7,)),
            dma((7,)),
        ],
        compiler_params=pltpu.CompilerParams(
            collective_id=0, has_side_effects=True, vmem_limit_bytes=VLIM * 2**20
        ),
        name="slab",
    )(
        edge_up.transpose(1, 2, 0).reshape(rows, gamma),
        corner,
        edge_left.transpose(1, 0, 2),
        doubled.reshape(dk * dl // 16, 16, dl * dl),
        panel.transpose(0, 2, 1),
    )


def general(corner, edge_up, edge_left, doubled, panel):
    dl, alpha_local = edge_up.shape[1], edge_up.shape[2]
    quad = doubled.reshape(dl, dl, dl, dl)
    partials = lax.dot_general(
        edge_up, corner, (((0,), (0,)), ((), ())), preferred_element_type=F32
    )
    corner_edge = lax.psum(partials, "col").astype(BF)
    grown = lax.dot_general(
        corner_edge,
        lax.all_gather(edge_left, "row", axis=0, tiled=True),
        (((2,), (0,)), ((), ())),
        preferred_element_type=F32,
    ).astype(BF)
    slab = lax.dot_general(
        quad, grown, (((0, 1), (0, 2)), ((), ())), preferred_element_type=F32
    ).astype(BF)
    partial_product = lax.dot_general(
        slab,
        lax.all_gather(panel, "row", axis=2, tiled=True),
        (((1, 3), (0, 1)), ((), ())),
        preferred_element_type=F32,
    )
    own_cols = lax.psum_scatter(partial_product, "col", scatter_dimension=2, tiled=True).astype(BF)
    rows_all = lax.all_gather(own_cols, "col", axis=2, tiled=True)
    total_rows = dl * alpha_local * lax.axis_size("row")
    gram = lax.psum_scatter(
        (
            lax.dot_general(
                rows_all, own_cols, (((0, 1), (0, 1)), ((), ())), preferred_element_type=F32
            )
            / total_rows
        ).astype(BF),
        "row",
        scatter_dimension=0,
        tiled=True,
    ).astype(F32)
    return (slab, own_cols, gram)


def local(corner, edge_up, edge_left, doubled, panel):
    n_row, n_col = lax.axis_size("row"), lax.axis_size("col")
    if (n_row, n_col) != (8, 4):
        return general(corner, edge_up, edge_left, doubled, panel)
    dl, alpha = edge_up.shape[1], edge_up.shape[2]
    slab, cols, gram = make_slab(edge_up, corner, edge_left, doubled, panel, dl * alpha * n_row)
    return (slab, cols.reshape(dl, alpha, -1), gram)


def solution(mesh):
    in_specs = (
        P("col", None),
        P("col", None, "row"),
        P("row", None, "col"),
        P(),
        P(None, "col", "row"),
    )
    out_specs = (P(None, None, "row", "col"), P(None, "row", "col"), P("row", "col"))
    return jax.shard_map(local, mesh=mesh, in_specs=in_specs, out_specs=out_specs, check_vma=False)
```
